32 devices in a mesh: groups: 2 (over y), wide: 4 (over z), narrow: 4 (over x, core).
Axes of the slice: x: 2, y: 2, z: 4, core: 2. Of those that a mesh axis runs over, the one named last changes fastest.
Arguments:
- residual: bfloat16 [512, 4096], P(('groups', 'wide')), parts along dimension 0, may hold values from -6 to 6
- query_rows: bfloat16 [512, 4096], P(('groups', 'wide'), 'narrow'), parts along dimension 0, may hold values from -160 to 160
- key_rows: bfloat16 [512, 4096], P(('groups', 'wide'), 'narrow'), parts along dimension 0, may hold values from -160 to 160
- value_rows: bfloat16 [512, 4096], P(('groups', 'wide'), 'narrow'), parts along dimension 0, may hold values from -6 to 6
- segment_ids: int32 [8, 64], P(('groups', 'wide')), parts along dimension 0, may hold values from 0 to 3, never falling along the last dimension, each value on 1 to 32 neighbouring positions
- o_weight: bfloat16 [4096, 4096], P('narrow', 'wide'), may hold values from -0.09375 to 0.09375
- norm_gain: float32 [4096], replicated, may hold values from 0.1 to 1.9
- w_gate: bfloat16 [32, 4096, 1024], P('wide', None, 'narrow'), may hold values from -0.09375 to 0.09375
- w_up: bfloat16 [32, 4096, 1024], P('wide', None, 'narrow'), may hold values from -0.09375 to 0.09375
- w_down: bfloat16 [32, 1024, 4096], P('wide', None, 'narrow'), may hold values from -0.1875 to 0.1875
- expert_ids: int32 [512, 8], P(('groups', 'wide')), parts along dimension 0, may hold values from 0 to 31, all different within a row; in each aligned block of 16 rows (0 to 15, 16 to 31, ...) at most 8 rows name the same one
- gate_weights: float32 [512, 8], P(('groups', 'wide')), parts along dimension 0, may hold values from 0.05 to 1
- target: bfloat16 [512, 4096], P(('groups', 'wide', 'narrow')), parts along dimension 0, may hold values from -6 to 6
Outputs:
- errors: float32 [512], P(('groups', 'wide', 'narrow')), parts along dimension 0
The draws below stay inside these ranges and needn't reach their ends.
There are 2 independent parts, one for each index of `groups`. The reference program is written for one: setup_inputs(seed, part) draws one part's arguments, and reference() takes and returns one part's arrays. A program takes and returns all parts, laid end to end along the dimension named above; an argument that names none is the same for every part. Nothing has to cross between parts.
Inputs may be any that keep to these rules, and one draw needn't show every extreme that they name: `expert_ids`: in each aligned block of 16 rows (the rows of one device) no expert is named more than 8 times, a bound that some block reaches. `segment_ids`: along each row the trajectory number never falls; a trajectory covers 1 to 32 positions.
All inputs are finite; a program needn't handle non-finite values.
Results may differ from the reference program's by a relative error of at most 0.0005.
Values may be sent and summed in bfloat16 or wider, within the bound.
No kernel may reach another device: no remote copies, remote signals or barrier semaphores. Data moves between devices by JAX's collectives and lax.ppermute only.
A program may use at most 128 MiB of HBM per device.

```python
import math
import jax
import jax.numpy as jnp
import numpy as np
from jax import lax

D = 4096
HEADS = 32
HD = 128
EXP_HID = 1024
EXPERTS = 32
TOP = 8
T_W = 64
ROWS = 16
CAP = 8
TOKENS = 256
N_WIDE = 4
N_NARROW = 4


def paired_draw(key):
    shape_pair = (TOKENS, HEADS * HD)
    query_base = jax.random.normal(jax.random.fold_in(key, 11), shape_pair, jnp.float32)
    key_base = jax.random.normal(jax.random.fold_in(key, 12), shape_pair, jnp.float32)
    return (jnp.clip(query_base, -160.0, 160.0), jnp.clip(key_base, -160.0, 160.0))


def draw_query_rows(key, part):
    return paired_draw(key)[0].astype(jnp.bfloat16)


def draw_key_rows(key, part):
    return paired_draw(key)[1].astype(jnp.bfloat16)


def shard_levels(key, shape, pieces, smallest, high):
    def one(position, shards_of):
        heights = jax.random.uniform(jax.random.fold_in(jax.random.fold_in(key, 6), position), (shards_of,), jnp.float32, smallest / len(pieces), high / len(pieces))
        return jnp.repeat(jnp.exp(heights), shape[position] // shards_of).reshape((-1,) + (1,) * (len(shape) - position - 1))

    factor_of = one(*pieces[0])
    for cut in pieces[1:]:
        factor_of = factor_of * one(*cut)
    return factor_of


def length_profile(amount, total, limit, lean):
    weights = [(1 << 20) // math.isqrt(standing ** lean) + 1 for standing in range(2, amount + 1)]
    surplus, given = total - limit - (amount - 1), [1] * (amount - 1)
    while surplus > 0:
        candidates = [i for i in range(amount - 1) if given[i] < limit]
        whole, remaining = sum([weights[i] for i in candidates]), surplus
        for i in candidates:
            addition = min(limit - given[i], max(1, remaining * weights[i] // whole), surplus)
            given[i] = given[i] + addition
            surplus = surplus - addition
    return np.array([limit] + given)


def uneven(own_key, count, total, most, lean):
    if count == 2:
        one = jax.random.randint(own_key, (), max(1, total - most), min(most, total - 1) + 1)
        return jnp.stack([one, total - one])
    sizes = jnp.asarray(length_profile(count, total, most, lean), jnp.int32)
    pairs = (count - 1) // 2
    donor, sink = sizes[1:1 + 2 * pairs:2], sizes[2:2 + 2 * pairs:2]
    margin = jnp.minimum(donor - 1, most - sink)
    moved = jax.random.randint(jax.random.fold_in(own_key, 1), (pairs,), 0, 1 << 20) % (margin + 1)
    sizes = sizes.at[1:1 + 2 * pairs:2].set(donor - moved).at[2:2 + 2 * pairs:2].set(sink + moved)
    return sizes[jax.random.permutation(jax.random.fold_in(own_key, 2), count)]


def assign_block(key, own, number, rows, count, top, bound, lean):
    ranking = jax.random.permutation(key, count)
    crowded, common = shares(count, rows * top, bound, lean, True), shares(count, rows * top, bound, lean, False)
    places = jnp.arange(count)

    def named(sizes, turn):
        used = int((sizes > 0).sum())
        fixed = max(1, used // 4)
        passed = fixed + (places - fixed + turn * (used - fixed)) % max(1, count - fixed)
        return jnp.zeros((count,), jnp.int32).at[ranking[jnp.where(places < fixed, places, passed)]].set(jnp.asarray(sizes, jnp.int32))

    sizes = jnp.where(number % 4 == 0, named(crowded, number // 4), named(common, number - number // 4 - 1))
    mixed = jax.random.permutation(jax.random.fold_in(own, 3), count)
    giver, taker = mixed[0:count // 2 * 2:2], mixed[1:count // 2 * 2:2]
    margin = jnp.minimum(sizes[giver] - 1, bound - sizes[taker]) // 2
    margin = jnp.where((giver == ranking[0]) | (taker == ranking[0]) | (sizes[taker] == 0), 0, jnp.maximum(margin, 0))
    passed = jax.random.randint(jax.random.fold_in(own, 4), (count // 2,), 0, 1 << 20) % (margin + 1)
    sizes = sizes.at[giver].add(-passed).at[taker].add(passed)
    labels = jnp.searchsorted(jnp.cumsum(sizes), jnp.arange(rows * top), side="right").astype(jnp.int32)
    table = labels.reshape(top, rows).T
    table = table[jax.random.permutation(jax.random.fold_in(own, 1), rows)]
    turn = jax.random.randint(jax.random.fold_in(own, 2), (rows, 1), 0, top)
    return jnp.take_along_axis(table, (jnp.arange(top)[None, :] + turn) % top, axis=1)


def shares(number_of, total, limit, slope, full):
    portions = [(1 << 20) // math.isqrt(grade ** slope) + 1 for grade in range(1, number_of + 1)]
    largest = limit if full else min(limit, max(-(-total // number_of), total * portions[0] // sum(portions)))
    least = 1 if total - largest >= number_of - 1 else 0
    given, surplus = [largest] + [least] * (number_of - 1), total - largest - least * (number_of - 1)
    while surplus > 0:
        candidates = [i for i in range(1, number_of) if given[i] < largest] or [i for i in range(1, number_of) if given[i] < limit]
        pool, remaining = sum([portions[i] for i in candidates]), surplus
        for i in candidates:
            addition = min(limit - given[i], max(1, remaining * portions[i] // pool), surplus)
            given[i] = given[i] + addition
            surplus = surplus - addition
    return np.array(given)


def gaussian(rng, extent, deviation, reach, pieces=(), held_as=jnp.bfloat16):
    result = jax.random.normal(rng, extent, jnp.float32) * deviation
    if len(pieces) > 0:
        result = shard_levels(rng, extent, pieces, -0.22, 0.18) * result
    return jnp.clip(result, min=-reach, max=reach).astype(held_as)


def setup_inputs(seed: int = 0, part: int = 0) -> dict:
    seeds = jax.random.split(jax.random.key(seed), 14)
    own_keys = jax.random.split(jax.random.fold_in(seeds[13], part), 14)
    residual = gaussian(own_keys[0], (TOKENS, D), 1.0, 6.0, ((0, 4),))
    query_rows = draw_query_rows(jax.random.fold_in(jax.random.fold_in(seeds[13], part), 71), part)
    key_rows = draw_key_rows(jax.random.fold_in(jax.random.fold_in(seeds[13], part), 71), part)
    value_rows = gaussian(own_keys[3], (TOKENS, HEADS * HD), 1.0, 6.0, ((0, 4), (1, 4)))
    segment_ids = jax.vmap(lambda own: jnp.searchsorted(jnp.cumsum(uneven(own, max(4, T_W // 16), T_W, T_W // 2, 1)), jnp.arange(T_W), side="right"))(jax.random.split(own_keys[4], N_WIDE)).reshape((N_WIDE, T_W)).astype(jnp.int32)
    o_weight = gaussian(seeds[5], (HEADS * HD, D), (HEADS * HD) ** -0.5, 0.09375, ((0, 4), (1, 4)))
    norm_gain = jnp.clip(1.0 + 0.18 * jax.random.normal(seeds[6], (D,), jnp.float32), 0.1, 1.9)
    w_gate = gaussian(seeds[7], (EXPERTS, D, EXP_HID), D ** -0.5, 0.09375, ((0, 4), (2, 4)))
    w_up = gaussian(seeds[8], (EXPERTS, D, EXP_HID), D ** -0.5, 0.09375, ((0, 4), (2, 4)))
    w_down = gaussian(seeds[9], (EXPERTS, EXP_HID, D), EXP_HID ** -0.5, 0.1875, ((0, 4), (2, 4)))
    expert_ids_keys = jax.random.split(jax.random.fold_in(own_keys[10], 1), TOKENS // ROWS)
    expert_ids_turns = jax.random.permutation(jax.random.fold_in(own_keys[10], 3), TOKENS // ROWS)
    expert_ids = jax.vmap(lambda own, number: assign_block(jax.random.fold_in(own_keys[10], 2), own, number, ROWS, EXPERTS, TOP, CAP, 2))(expert_ids_keys, expert_ids_turns).reshape((TOKENS, TOP))
    gate_weights = jnp.clip(jnp.exp(math.log(1.0) - 2.9957323 * jax.random.uniform(own_keys[11], (TOKENS, TOP), jnp.float32) ** shard_levels(own_keys[11], (TOKENS, TOP), ((0, 4),), -0.2, 0.2)), 0.05, 1.0)
    target = gaussian(own_keys[12], (TOKENS, D), 1.0, 6.0, ((0, 16),))
    return {"residual": residual, "query_rows": query_rows, "key_rows": key_rows, "value_rows": value_rows, "segment_ids": segment_ids, "o_weight": o_weight, "norm_gain": norm_gain, "w_gate": w_gate, "w_up": w_up, "w_down": w_down, "expert_ids": expert_ids, "gate_weights": gate_weights, "target": target}


def attend(query_block, key_block, value_block, seg_row):
    tok_count = query_block.shape[0]
    head_count = query_block.shape[1] // HD
    query_heads = query_block.reshape(tok_count, head_count, HD).astype(jnp.float32)
    key_heads = key_block.reshape(tok_count, head_count, HD).astype(jnp.float32)
    value_heads = value_block.reshape(tok_count, head_count, HD).astype(jnp.float32)
    scores = jnp.einsum('qhd,khd->hqk', query_heads, key_heads) * HD ** (-0.5)
    places = jnp.arange(tok_count, dtype=jnp.int32)
    allowed = (seg_row[:, None] == seg_row[None, :]) & (places[None, :] <= places[:, None])
    scores = jnp.where(allowed[None], scores, -jnp.inf)
    peak_score = lax.optimization_barrier(jnp.max(scores, axis=2, keepdims=True))
    weights = jnp.exp(scores - peak_score)
    denom_sum = lax.optimization_barrier(jnp.sum(weights, axis=2, keepdims=True))
    weights_b = weights.astype(jnp.bfloat16).astype(jnp.float32)
    mixed_out = jnp.einsum('hqk,khd->qhd', weights_b, value_heads) / jnp.transpose(denom_sum, (1, 0, 2))
    return mixed_out.reshape(tok_count, -1).astype(jnp.bfloat16)

def normalize(stream_rows, gain_vector):
    mean_sq = lax.optimization_barrier(jnp.mean(stream_rows * stream_rows, axis=1, keepdims=True))
    return (stream_rows * lax.rsqrt(mean_sq + 1e-06) * gain_vector.astype(jnp.float32)).astype(jnp.bfloat16)

def reference(residual, query_rows, key_rows, value_rows, segment_ids, o_weight, norm_gain, w_gate, w_up, w_down, expert_ids, gate_weights, target):
    model_width = residual.shape[1]
    blocks = (query_rows.reshape(N_WIDE, T_W, -1), key_rows.reshape(N_WIDE, T_W, -1), value_rows.reshape(N_WIDE, T_W, -1), segment_ids)
    attended = lax.map(lambda block_args: attend(*block_args), blocks).reshape(TOKENS, -1)
    mix_sum = jnp.dot(attended, o_weight, preferred_element_type=jnp.float32)
    stream = residual.astype(jnp.float32) + mix_sum
    normed = normalize(stream, norm_gain)
    flat_ids = expert_ids.reshape(-1).astype(jnp.int32)
    order = jnp.argsort(flat_ids, stable=True).astype(jnp.int32)
    sorted_ids = flat_ids[order]
    onehot = (flat_ids[:, None] == jnp.arange(EXPERTS, dtype=jnp.int32)[None, :]).astype(jnp.int32)
    counts = lax.optimization_barrier(jnp.sum(onehot, axis=0))
    starts = (jnp.cumsum(counts) - counts).astype(jnp.int32)
    most_load = N_WIDE * N_NARROW * CAP
    sorted_rows = normed[order // TOP]
    padded = jnp.concatenate([sorted_rows, jnp.zeros((most_load, model_width), sorted_rows.dtype)], axis=0)

    def expert_pass(expert_args):
        first_row, gate_mat, up_mat, down_mat = expert_args
        block_rows = lax.dynamic_slice_in_dim(padded, first_row, most_load, 0)
        gate_val = jnp.dot(block_rows, gate_mat, preferred_element_type=jnp.float32)
        up_val = jnp.dot(block_rows, up_mat, preferred_element_type=jnp.float32)
        hidden = (jax.nn.silu(gate_val) * up_val).astype(jnp.bfloat16)
        return jnp.dot(hidden, down_mat, preferred_element_type=jnp.float32).astype(jnp.bfloat16)
    results = lax.map(expert_pass, (starts, w_gate, w_up, w_down))
    local_index = (jnp.arange(TOKENS * TOP, dtype=jnp.int32) - starts[sorted_ids]).astype(jnp.int32)
    sorted_out = results.reshape(EXPERTS * most_load, -1)[sorted_ids * most_load + local_index]
    per_route = jnp.zeros_like(sorted_out).at[order].set(sorted_out).reshape(TOKENS, TOP, -1)
    moe_sum = lax.optimization_barrier(jnp.sum(gate_weights.astype(jnp.float32)[:, :, None] * per_route.astype(jnp.float32), axis=1))
    predicted = stream + moe_sum
    return lax.optimization_barrier(jnp.mean((predicted - target.astype(jnp.float32)) ** 2, axis=1))
```

```python
import functools

import jax
import jax.numpy as jnp
from jax import lax
from jax.experimental import pallas as pl
from jax.experimental.pallas import tpu as pltpu
from jax.sharding import PartitionSpec as P

HD = 128
EXPERTS = 32
TOP = 8
BF16 = jnp.bfloat16
F32 = jnp.float32


def whole(shape, space=pltpu.VMEM):
    rank = len(shape)
    return pl.BlockSpec(shape, lambda *_: (0,) * rank, pipeline_mode=pl.Buffered(1))


def dot(a, b, dims=((1,), (0,))):
    return lax.dot_general(a, b, (dims, ((), ())), preferred_element_type=F32)


def each(count, step):
    if count == 1:
        step(0)
    else:
        lax.fori_loop(0, count, lambda i, carry: (step(i), carry)[1], 0)


def chunk_of(total, most):
    return most if total % most == 0 else total


def wide_pieces(rows):
    count = lax.axis_size("wide")
    me = lax.axis_index("wide")
    if count > 8:
        return [lax.all_gather(rows, "wide", axis=0)], jnp.arange(count, dtype=jnp.int32)
    found = [rows[None]]
    for step in range(1, count):
        found.append(lax.ppermute(rows, "wide", [((i + step) % count, i) for i in range(count)])[None])
    return found, (me + jnp.arange(count, dtype=jnp.int32)) % count


def wide_exchange(block_of):
    count = lax.axis_size("wide")
    me = lax.axis_index("wide")
    if count > 8:
        stacked = jnp.stack([block_of(i) for i in range(count)])
        return [lax.all_to_all(stacked, "wide", split_axis=0, concat_axis=0, tiled=True)]
    found = [block_of(me)[None]]
    for step in range(1, count):
        pairs = [((i + step) % count, i) for i in range(count)]
        found.append(lax.ppermute(block_of((me - step) % count), "wide", pairs)[None])
    return found


def narrow_flip(rows, bit):
    count = lax.axis_size("narrow")
    return lax.ppermute(rows, "narrow", [(i, i ^ bit) for i in range(count)])


def narrow_pieces(rows):
    count = lax.axis_size("narrow")
    held = {0: rows}
    bit = count // 2
    while bit:
        for j in list(held):
            held[j ^ bit] = narrow_flip(held[j], bit)
        bit //= 2
    return [held[j] for j in range(count)]


def attend_kernel(q_ref, k_ref, v_ref, seg_ref, out_ref):
    tok_count, width = q_ref.shape
    seg = jnp.broadcast_to(seg_ref[...].astype(F32), (tok_count, tok_count))
    key_pos = lax.broadcasted_iota(jnp.int32, (tok_count, tok_count), 1)
    query_pos = lax.broadcasted_iota(jnp.int32, (tok_count, tok_count), 0)
    allowed = (seg == seg.T) & (key_pos <= query_pos)
    for h in range(width // HD):
        cols = slice(h * HD, (h + 1) * HD)
        scores = dot(q_ref[:, cols], k_ref[:, cols], ((1,), (1,))) * HD ** (-0.5)
        scores = jnp.where(allowed, scores, -jnp.inf)
        weights = jnp.exp(scores - jnp.max(scores, axis=1, keepdims=True))
        denom = jnp.sum(weights, axis=1, keepdims=True)
        out_ref[:, cols] = (dot(weights.astype(BF16), v_ref[:, cols]) / denom).astype(BF16)


def attend(q, k, v, seg):
    return pl.pallas_call(attend_kernel, out_shape=jax.ShapeDtypeStruct(q.shape, BF16), name="attend")(q, k, v, seg)


def project_kernel(place_ref, *refs, pieces, n_count):
    att, w_ref, outs, product_ref = refs[:pieces], refs[pieces], refs[pieces + 1 : -1], refs[-1]
    me = place_ref[0]
    rows = jnp.concatenate([a[i] for a in att for i in range(a.shape[0])], axis=0)
    product_ref[...] = dot(rows, w_ref[...]).reshape(product_ref.shape)

    def spread(i, carry):
        w = place_ref[1 + i]
        for j in range(n_count):
            outs[j][w] = product_ref[i, me ^ j].astype(outs[j].dtype)
        return carry

    lax.fori_loop(0, product_ref.shape[0], spread, 0)


def project(place, att, o_weight, n_count):
    w_count = sum(a.shape[0] for a in att)
    tok_count, width = att[0].shape[1], o_weight.shape[1]
    shape = (w_count, tok_count // n_count, width)
    outs = [jax.ShapeDtypeStruct(shape, F32 if j == 0 else BF16) for j in range(n_count)]
    return pl.pallas_call(
        functools.partial(project_kernel, pieces=len(att), n_count=n_count),
        grid_spec=pltpu.PrefetchScalarGridSpec(
            num_scalar_prefetch=1,
            grid=(1,),
            in_specs=[whole(a.shape) for a in att] + [whole(o_weight.shape)],
            out_specs=[whole(shape) for _ in outs],
            scratch_shapes=[pltpu.VMEM((w_count, n_count, *shape[1:]), F32)],
        ),
        out_shape=outs,
        name="project",
    )(place, *att, o_weight)


def stream_kernel(place_ref, gain_ref, *refs, parts, pieces):
    shares, resid, out_ref = refs[:parts], refs[parts : parts + pieces], refs[parts + pieces]
    index = 0
    for a in resid:
        for i in range(a.shape[0]):
            w = place_ref[1 + index]
            index += 1
            total = a[i].astype(F32)
            for s in shares:
                total = total + s[w].astype(F32)
            out_ref[w] = (total * gain_ref[...]).astype(BF16)


def stream_of(place, gain_here, shares, resid):
    shape = shares[0].shape
    return pl.pallas_call(
        functools.partial(stream_kernel, parts=len(shares), pieces=len(resid)),
        grid_spec=pltpu.PrefetchScalarGridSpec(
            num_scalar_prefetch=1,
            grid=(1,),
            in_specs=[whole(gain_here.shape)] + [whole(a.shape) for a in (*shares, *resid)],
            out_specs=whole(shape),
        ),
        out_shape=jax.ShapeDtypeStruct(shape, BF16),
        name="stream",
    )(place, gain_here, *shares, *resid)


def hidden_kernel(place_ref, slot_ref, gain_ref, target_ref, *refs, counts, n_count):
    total = len(counts) * n_count
    pieces, (wg_ref, wu_ref, out_ref, base_ref, rows_ref, scale_ref, hidden_ref) = refs[:total], refs[total:]
    expert = pl.program_id(0)
    block = pieces[0].shape[1]
    width = pieces[0].shape[2]
    tokens, model_width = rows_ref.shape

    @pl.when(expert == 0)
    def _():
        first = 1
        for a, count in enumerate(counts):

            def place(i, a=a, first=first):
                col = pl.multiple_of(place_ref[first + i] * width, 128)
                for j in range(n_count):
                    rows_ref[j * block : (j + 1) * block, pl.ds(col, width)] = pieces[a * n_count + j][i]

            each(count, place)
            first += count
        inverse = 1.0 / gain_ref[...]
        some = chunk_of(tokens, 64)

        def scale_rows(c):
            here = pl.ds(pl.multiple_of(c * some, 16), some)
            stream = rows_ref[here, :].astype(F32) * inverse
            mean_sq = jnp.sum(stream * stream, axis=1, keepdims=True) / model_width
            scale_ref[here, :] = jnp.broadcast_to(lax.rsqrt(mean_sq + 1e-06), (some, 128))

        each(tokens // some, scale_rows)
        part = target_ref.shape[0]
        first = pl.multiple_of(place_ref[0] * part, 8)
        own = rows_ref[pl.ds(first, part), :].astype(F32) * inverse
        base_ref[...] = own - target_ref[...].astype(F32)

    many = chunk_of(tokens, 256)

    def rows_done(c):
        here = pl.ds(pl.multiple_of(c * many, 16), many)
        rows = rows_ref[here, :]
        scale = scale_ref[here, :1]
        gate_val = dot(rows, wg_ref[0]) * scale
        up_val = dot(rows, wu_ref[0]) * scale
        hidden_ref[here, :] = (gate_val / (1.0 + jnp.exp(-gate_val)) * up_val).astype(BF16)

    each(tokens // many, rows_done)
    slots = out_ref.shape[1]
    few = chunk_of(slots, 128)

    def slots_done(c):
        first = pl.multiple_of(c * few, 16)
        slot = jnp.broadcast_to(slot_ref[0], (few, tokens))
        chosen = (lax.broadcasted_iota(jnp.int32, slot.shape, 0) + first == slot).astype(F32).astype(BF16)
        out_ref[0, pl.ds(first, few), :] = dot(chosen, hidden_ref[...]).astype(BF16)

    each(slots // few, slots_done)


def hidden_of(place, slot, gain, target, pieces, w_gate, w_up, slots):
    n_count = len(pieces[0])
    experts, model_width, hid = w_gate.shape
    flat = [p for group in pieces for p in group]
    tokens = flat[0].shape[1] * n_count
    weight = pl.BlockSpec((1, model_width, hid), lambda e, *_: (e, 0, 0))
    return pl.pallas_call(
        functools.partial(hidden_kernel, counts=[g[0].shape[0] for g in pieces], n_count=n_count),
        grid_spec=pltpu.PrefetchScalarGridSpec(
            num_scalar_prefetch=1,
            grid=(experts,),
            in_specs=[pl.BlockSpec((1, 1, tokens), lambda e, *_: (e, 0, 0)), whole(gain.shape), whole(target.shape)]
            + [whole(p.shape) for p in flat]
            + [weight, weight],
            out_specs=[pl.BlockSpec((1, slots, hid), lambda e, *_: (e, 0, 0)), whole(target.shape)],
            scratch_shapes=[
                pltpu.VMEM((tokens, model_width), BF16),
                pltpu.VMEM((tokens, 128), F32),
                pltpu.VMEM((tokens, hid), BF16),
            ],
        ),
        out_shape=[jax.ShapeDtypeStruct((experts, slots, hid), BF16), jax.ShapeDtypeStruct(target.shape, F32)],
        name="hidden",
    )(place, slot, gain, target, *flat, w_gate, w_up)


def combine_kernel(place_ref, slot_ref, gate_ref, *refs, n_count):
    hidden, (wd_ref, out_ref, sum_ref, result_ref) = refs[:n_count], refs[n_count:]
    expert = pl.program_id(0)
    me = place_ref[0]
    slots, hid = hidden[0].shape[1:]

    @pl.when(expert == 0)
    def _():
        sum_ref[...] = jnp.zeros_like(sum_ref)

    few = chunk_of(slots, 128)

    def slots_done(c):
        here = pl.ds(pl.multiple_of(c * few, 16), few)
        result = None
        for j in range(n_count):
            first = pl.multiple_of((me ^ j) * hid, 128)
            part = dot(hidden[j][0, here, :], wd_ref[0, pl.ds(first, hid), :])
            result = part if result is None else result + part
        result_ref[here, :] = result.astype(BF16)

    each(slots // few, slots_done)
    tokens = sum_ref.shape[0]
    many = chunk_of(tokens, 256)

    def rows_done(c):
        here = pl.ds(pl.multiple_of(c * many, 128), many)
        slot = jnp.broadcast_to(slot_ref[0, :, here], (slots, many))
        gate = jnp.broadcast_to(gate_ref[0, :, here], (slots, many))
        weight = jnp.where(lax.broadcasted_iota(jnp.int32, slot.shape, 0) == slot, gate, 0.0)
        high = weight.astype(BF16)
        low = (weight - high.astype(F32)).astype(BF16)
        result = result_ref[...]
        sum_ref[here, :] += dot(high, result, ((0,), (0,))) + dot(low, result, ((0,), (0,)))

    each(tokens // many, rows_done)

    @pl.when(expert == pl.num_programs(0) - 1)
    def _():
        out_ref[...] = sum_ref[...].astype(BF16)


def combine(place, slot, gate, hidden, w_down):
    n_count = len(hidden)
    experts, slots, hid = hidden[0].shape
    tokens, width = slot.shape[2], w_down.shape[2]
    row = pl.BlockSpec((1, 1, tokens), lambda e, *_: (e, 0, 0))
    return pl.pallas_call(
        functools.partial(combine_kernel, n_count=n_count),
        grid_spec=pltpu.PrefetchScalarGridSpec(
            num_scalar_prefetch=1,
            grid=(experts,),
            in_specs=[row, row]
            + [pl.BlockSpec((1, slots, hid), lambda e, *_: (e, 0, 0)) for _ in hidden]
            + [pl.BlockSpec((1, hid * n_count, width), lambda e, *_: (e, 0, 0))],
            out_specs=whole((tokens, width)),
            scratch_shapes=[pltpu.VMEM((tokens, width), F32), pltpu.VMEM((slots, width), BF16)],
        ),
        out_shape=jax.ShapeDtypeStruct((tokens, width), BF16),
        name="combine",
    )(place, slot, gate, *hidden, w_down)


def routing(idx, packed, experts):
    stacked = jnp.concatenate(packed, axis=0)
    stacked = jnp.zeros_like(stacked).at[idx].set(stacked) if len(packed) == 1 else roll_wide(stacked)
    ids = stacked[:, :TOP].transpose(1, 0, 2).reshape(TOP, -1)
    gates = stacked[:, TOP:].transpose(1, 0, 2).reshape(TOP, -1)
    first = (lax.axis_index("wide") * experts).astype(F32)
    names = first + jnp.arange(experts, dtype=F32)
    same = ids[None] == names[:, None, None]
    member = jnp.any(same, axis=1)
    gate = jnp.sum(jnp.where(same, gates[None], 0.0), axis=1)
    tokens = ids.shape[1]
    before = (jnp.arange(tokens)[:, None] < jnp.arange(tokens)[None, :]).astype(BF16)
    rank = dot(member.astype(BF16), before).astype(jnp.int32)
    return jnp.where(member, rank, -1), gate


def roll_wide(stacked):
    count = stacked.shape[0]
    me = lax.axis_index("wide")
    return lax.dynamic_slice_in_dim(jnp.concatenate([stacked, stacked], axis=0), (count - me) % count, count, 0)


def body(
    residual,
    query_rows,
    key_rows,
    value_rows,
    segment_ids,
    o_weight,
    norm_gain,
    w_gate,
    w_up,
    w_down,
    expert_ids,
    gate_weights,
    target,
):
    w_count = lax.axis_size("wide")
    n_count = lax.axis_size("narrow")
    w_here = lax.axis_index("wide")
    n_here = lax.axis_index("narrow")
    tok_count, model_width = residual.shape
    part = tok_count // n_count
    experts = w_gate.shape[0]
    capacity = max(2, 2 * part * TOP // EXPERTS)
    slots = w_count * n_count * capacity
    out_width = o_weight.shape[1]

    attended = attend(query_rows, key_rows, value_rows, segment_ids)
    att_pieces, w_index = wide_pieces(attended)
    n_place = jnp.concatenate([n_here[None].astype(jnp.int32), w_index])
    w_place = jnp.concatenate([w_here[None].astype(jnp.int32), w_index])

    packed = jnp.concatenate([expert_ids.astype(F32).T, gate_weights.T], axis=0)
    packed_pieces, _ = wide_pieces(packed)
    slot, gate = routing(w_index, packed_pieces, experts)
    by_place = slot.reshape(experts, w_count, n_count, part)
    slot_near = jnp.stack(
        [lax.dynamic_index_in_dim(by_place, n_here ^ j, 2, keepdims=False) for j in range(n_count)], axis=1
    ).reshape(experts, 1, -1)

    own_resid = lax.dynamic_slice_in_dim(residual, n_here * part, part, 0)
    resid_pieces = wide_exchange(lambda w: lax.dynamic_slice_in_dim(own_resid, w * out_width, out_width, 1))

    shares = project(n_place, att_pieces, o_weight, n_count)
    shares = [shares[0]] + [narrow_flip(shares[j], j) for j in range(1, n_count)]
    gain_here = lax.dynamic_slice_in_dim(norm_gain, w_here * out_width, out_width, 0)[None]
    scaled = stream_of(n_place, gain_here, shares, resid_pieces).reshape(w_count * part, out_width)

    wide_rows, _ = wide_pieces(scaled)
    pieces = [narrow_pieces(rows) for rows in wide_rows]
    hidden, base = hidden_of(w_place, slot_near, norm_gain[None], target, pieces, w_gate, w_up, slots)
    hidden = narrow_pieces(hidden)
    partial_sum = combine(n_place, slot[:, None], gate[:, None], hidden, w_down)
    returned = lax.all_to_all(
        partial_sum.reshape(w_count * n_count, part, -1),
        ("wide", "narrow"),
        split_axis=0,
        concat_axis=0,
        tiled=True,
    ).reshape(w_count, n_count, part, -1)
    moe_sum = jnp.sum(returned.astype(F32), axis=0).transpose(1, 0, 2)
    miss = base.reshape(moe_sum.shape) + moe_sum
    return jnp.sum(miss * miss, axis=(1, 2)) / model_width


def solution(mesh):
    return jax.shard_map(
        body,
        mesh=mesh,
        in_specs=(
            P(("groups", "wide"), None),
            P(("groups", "wide"), "narrow"),
            P(("groups", "wide"), "narrow"),
            P(("groups", "wide"), "narrow"),
            P(("groups", "wide"), None),
            P("narrow", "wide"),
            P(),
            P("wide", None, "narrow"),
            P("wide", None, "narrow"),
            P("wide", None, "narrow"),
            P(("groups", "wide"), None),
            P(("groups", "wide"), None),
            P(("groups", "wide", "narrow"), None),
        ),
        out_specs=P(("groups", "wide", "narrow")),
        check_vma=False,
    )
```

```python
import functools

import jax
import jax.numpy as jnp
from jax import lax
from jax.experimental import pallas as pl
from jax.experimental.pallas import tpu as pltpu
from jax.sharding import PartitionSpec as P


HD = 128
EXPERTS = 32
TOP = 8
BF16 = jnp.bfloat16
F32 = jnp.float32
PARTS = 2


def whole(shape):
    rank = len(shape)
    return pl.BlockSpec(shape, lambda *_: (0,) * rank, pipeline_mode=pl.Buffered(1))


def dot(a, b, dims=((1,), (0,))):
    return lax.dot_general(a, b, (dims, ((), ())), preferred_element_type=F32)


def each(count, step):
    if count == 1:
        step(0)
    else:
        lax.fori_loop(0, count, lambda i, carry: (step(i), carry)[1], 0)


def chunk_of(total, most):
    return most if total % most == 0 else total


def wide_pieces(rows):
    count = lax.axis_size("wide")
    me = lax.axis_index("wide")
    if count > 8:
        return [lax.all_gather(rows, "wide", axis=0)], jnp.arange(count, dtype=jnp.int32)
    found = [rows[None]]
    for step in range(1, count):
        found.append(lax.ppermute(rows, "wide", [((i + step) % count, i) for i in range(count)])[None])
    return found, (me + jnp.arange(count, dtype=jnp.int32)) % count


def wide_exchange(block_of, after):
    count = lax.axis_size("wide")
    me = lax.axis_index("wide")
    if count > 8:
        stacked = jnp.stack([block_of(i) for i in range(count)])
        return [lax.all_to_all(stacked, "wide", split_axis=0, concat_axis=0, tiled=True)]
    found = [block_of(me)[None]]
    blocks, _ = lax.optimization_barrier(([block_of((me - step) % count) for step in range(1, count)], after))
    for step in range(1, count):
        pairs = [((i + step) % count, i) for i in range(count)]
        found.append(lax.ppermute(blocks[step - 1], "wide", pairs)[None])
    return found


def narrow_flip(rows, bit):
    count = lax.axis_size("narrow")
    return lax.ppermute(rows, "narrow", [(i, i ^ bit) for i in range(count)])


def narrow_pieces(rows, after=None):
    count = lax.axis_size("narrow")
    held = {0: rows}
    bit = count // 2
    while bit:
        for j in list(held):
            held[j ^ bit] = narrow_flip(held[j], bit)
        if after is not None and bit == count // 2:
            held[bit], after = lax.optimization_barrier((held[bit], after))
        bit //= 2
    return [held[j] for j in range(count)], after


def attend_kernel(q_ref, k_ref, v_ref, seg_ref, out_ref):
    tok_count, width = q_ref.shape
    seg = jnp.broadcast_to(seg_ref[...].astype(F32), (tok_count, tok_count))
    key_pos = lax.broadcasted_iota(jnp.int32, (tok_count, tok_count), 1)
    query_pos = lax.broadcasted_iota(jnp.int32, (tok_count, tok_count), 0)
    allowed = (seg == seg.T) & (key_pos <= query_pos)
    for h in range(width // HD):
        cols = slice(h * HD, (h + 1) * HD)
        scores = dot(q_ref[:, cols], k_ref[:, cols], ((1,), (1,))) * HD ** (-0.5)
        scores = jnp.where(allowed, scores, -jnp.inf)
        weights = jnp.exp(scores - jnp.max(scores, axis=1, keepdims=True))
        denom = jnp.sum(weights, axis=1, keepdims=True)
        out_ref[:, cols] = (dot(weights.astype(BF16), v_ref[:, cols]) / denom).astype(BF16)


def attend(q, k, v, seg):
    return pl.pallas_call(attend_kernel, out_shape=jax.ShapeDtypeStruct(q.shape, BF16), name="attend")(q, k, v, seg)


def project_kernel(place_ref, *refs, pieces, n_count):
    att, w_ref, outs, product_ref = refs[:pieces], refs[pieces], refs[pieces + 1 : -1], refs[-1]
    me = place_ref[0]
    rows = jnp.concatenate([a[i] for a in att for i in range(a.shape[0])], axis=0)
    product_ref[...] = dot(rows, w_ref[...]).reshape(product_ref.shape)

    def spread(i, carry):
        w = place_ref[1 + i]
        for j in range(n_count):
            outs[j][w] = product_ref[i, me ^ j].astype(outs[j].dtype)
        return carry

    lax.fori_loop(0, product_ref.shape[0], spread, 0)


def project(place, att, o_weight, n_count):
    w_count = sum(a.shape[0] for a in att)
    tok_count, width = att[0].shape[1], o_weight.shape[1]
    shape = (w_count, tok_count // n_count, width)
    outs = [jax.ShapeDtypeStruct(shape, F32 if j == 0 else BF16) for j in range(n_count)]
    return pl.pallas_call(
        functools.partial(project_kernel, pieces=len(att), n_count=n_count),
        grid_spec=pltpu.PrefetchScalarGridSpec(
            num_scalar_prefetch=1,
            grid=(1,),
            in_specs=[whole(a.shape) for a in att] + [whole(o_weight.shape)],
            out_specs=[whole(shape) for _ in outs],
            scratch_shapes=[pltpu.VMEM((w_count, n_count, *shape[1:]), F32)],
        ),
        out_shape=outs,
        name="project",
    )(place, *att, o_weight)


def stream_kernel(place_ref, gain_ref, *refs, parts, pieces):
    shares, resid, out_ref = refs[:parts], refs[parts : parts + pieces], refs[parts + pieces]
    index = 0
    for a in resid:
        for i in range(a.shape[0]):
            w = place_ref[1 + index]
            index += 1
            total = a[i].astype(F32)
            for s in shares:
                total = total + s[w].astype(F32)
            out_ref[w] = (total * gain_ref[...]).astype(BF16)


def stream_of(place, gain_here, shares, resid):
    shape = shares[0].shape
    return pl.pallas_call(
        functools.partial(stream_kernel, parts=len(shares), pieces=len(resid)),
        grid_spec=pltpu.PrefetchScalarGridSpec(
            num_scalar_prefetch=1,
            grid=(1,),
            in_specs=[whole(gain_here.shape)] + [whole(a.shape) for a in (*shares, *resid)],
            out_specs=whole(shape),
        ),
        out_shape=jax.ShapeDtypeStruct(shape, BF16),
        name="stream",
    )(place, gain_here, *shares, *resid)


def base_kernel(place_ref, gain_ref, target_ref, *refs):
    pieces, base_ref = refs[:-1], refs[-1]
    width = pieces[0].shape[2]
    part = target_ref.shape[0]
    for i, piece in enumerate(pieces):
        col = pl.multiple_of(place_ref[1 + i] * width, 128)
        own = piece[0, pl.ds(pl.multiple_of(place_ref[0] * part, 8), part), :].astype(F32)
        base_ref[:, pl.ds(col, width)] = own / gain_ref[:, pl.ds(col, width)] - target_ref[:, pl.ds(col, width)].astype(F32)


def base_of(place, gain, target, pieces):
    return pl.pallas_call(
        base_kernel,
        grid_spec=pltpu.PrefetchScalarGridSpec(
            num_scalar_prefetch=1,
            grid=(1,),
            in_specs=[whole(a.shape) for a in (gain, target, *pieces)],
            out_specs=whole(target.shape),
        ),
        out_shape=jax.ShapeDtypeStruct(target.shape, F32),
        name="base",
    )(place, gain, target, *pieces)


def hidden_kernel(place_ref, slot_ref, norm_ref, *refs, groups, first_call):
    total = sum(groups)
    pieces, wg_ref, wu_ref, out_ref = refs[:total], refs[total], refs[total + 1], refs[total + 2]
    rest = list(refs[total + 3 :])
    scale_ref = rest.pop(0) if first_call else norm_ref
    hidden_ref = rest.pop(0)
    tokens = scale_ref.shape[0]
    rows_ref = rest.pop(0) if total > 1 else pieces[0].at[0]
    model_width = wg_ref.shape[1]

    @pl.when(pl.program_id(0) == 0)
    def _():
        if total > 1:
            block, width = pieces[0].shape[1:]
            for i, count in enumerate(groups):
                col = pl.multiple_of(place_ref[1 + i] * width, 128)
                for j in range(count):
                    rows_ref[j * block : (j + 1) * block, pl.ds(col, width)] = pieces[i * count + j][0]
        if first_call:
            some = chunk_of(tokens, 64)
            wide = chunk_of(model_width, 1024)

            def scale_rows(c):
                here = pl.ds(pl.multiple_of(c * some, 16), some)
                sums = 0.0
                for first in range(0, model_width, wide):
                    inverse = 1.0 / norm_ref[:, first : first + wide]
                    stream = rows_ref[here, first : first + wide].astype(F32) * inverse
                    sums += jnp.sum(stream * stream, axis=1, keepdims=True)
                scale_ref[here, :] = jnp.broadcast_to(lax.rsqrt(sums / model_width + 1e-06), (some, 128))

            each(tokens // some, scale_rows)

    many = chunk_of(tokens, 256)

    def rows_done(c):
        here = pl.ds(pl.multiple_of(c * many, 128), many)
        rows = rows_ref[here, :]
        scale = scale_ref[here, :1]
        gate_val = dot(rows, wg_ref[0]) * scale
        up_val = dot(rows, wu_ref[0]) * scale
        hidden_ref[here, :] = (gate_val / (1.0 + jnp.exp(-gate_val)) * up_val).astype(BF16)

    each(tokens // many, rows_done)
    slots = out_ref.shape[1]
    few = chunk_of(slots, 128)

    def slots_done(c):
        first = pl.multiple_of(c * few, 16)
        slot = jnp.broadcast_to(slot_ref[0], (few, tokens))
        chosen = (lax.broadcasted_iota(jnp.int32, slot.shape, 0) + first == slot).astype(F32).astype(BF16)
        out_ref[0, pl.ds(first, few), :] = dot(chosen, hidden_ref[...]).astype(BF16)

    each(slots // few, slots_done)


def hidden_of(place, slot, norm, pieces, w_gate, w_up, slots, first, experts):
    model_width, hid = w_gate.shape[1:]
    flat = [p for group in pieces for p in group]
    tokens = slot.shape[2]
    weight = pl.BlockSpec((1, model_width, hid), lambda e, *_: (first + e, 0, 0))
    rows = [pltpu.VMEM((tokens, model_width), BF16)] if len(flat) > 1 else []
    out_specs = [pl.BlockSpec((1, slots, hid), lambda e, *_: (e, 0, 0))]
    out_shape = [jax.ShapeDtypeStruct((experts, slots, hid), BF16)]
    if first == 0:
        out_specs.append(whole((tokens, 128)))
        out_shape.append(jax.ShapeDtypeStruct((tokens, 128), F32))
    found = pl.pallas_call(
        functools.partial(hidden_kernel, groups=[len(g) for g in pieces], first_call=first == 0),
        grid_spec=pltpu.PrefetchScalarGridSpec(
            num_scalar_prefetch=1,
            grid=(experts,),
            in_specs=[pl.BlockSpec((1, 1, tokens), lambda e, *_: (first + e, 0, 0)), whole(norm.shape)]
            + [whole(p.shape) for p in flat]
            + [weight, weight],
            out_specs=out_specs,
            scratch_shapes=[pltpu.VMEM((tokens, hid), BF16)] + rows,
        ),
        out_shape=out_shape,
        name="hidden",
    )(place, slot, norm, *flat, w_gate, w_up)
    return found if first == 0 else (found[0], norm)


def combine_kernel(place_ref, slot_ref, gate_ref, *refs, n_count, started):
    hidden, weights, rest = refs[:n_count], refs[n_count : 2 * n_count], refs[2 * n_count :]
    out_ref, sum_ref, result_ref = rest[-3:]
    group, slots, _ = hidden[0].shape

    @pl.when(pl.program_id(0) == 0)
    def _():
        sum_ref[...] = rest[0][...] if started else jnp.zeros_like(sum_ref)

    few = chunk_of(slots, 128)
    for e in range(group):

        def slots_done(c, e=e):
            here = pl.ds(pl.multiple_of(c * few, 16), few)
            result = 0.0
            for j in range(n_count):
                result += dot(hidden[j][e, here, :], weights[j][e])
            result_ref[pl.ds(pl.multiple_of(e * slots + c * few, 16), few), :] = result.astype(BF16)

        each(slots // few, slots_done)
    tokens = sum_ref.shape[0]
    many = chunk_of(tokens, 256)

    def rows_done(c):
        here = pl.ds(pl.multiple_of(c * many, 128), many)
        weight = []
        for e in range(group):
            slot = jnp.broadcast_to(slot_ref[e, :, here], (slots, many))
            gate = jnp.broadcast_to(gate_ref[e, :, here], (slots, many))
            weight.append(jnp.where(lax.broadcasted_iota(jnp.int32, slot.shape, 0) == slot, gate, 0.0))
        weight = jnp.concatenate(weight, axis=0) if group > 1 else weight[0]
        high = weight.astype(BF16)
        low = (weight - high.astype(F32)).astype(BF16)
        result = result_ref[...]
        sum_ref[here, :] += dot(high, result, ((0,), (0,))) + dot(low, result, ((0,), (0,)))

    each(tokens // many, rows_done)

    @pl.when(pl.program_id(0) == pl.num_programs(0) - 1)
    def _():
        out_ref[...] = sum_ref[...].astype(out_ref.dtype)


def combine(place, slot, gate, hidden, w_down, first, so_far, out_type):
    n_count = len(hidden)
    experts, slots, hid = hidden[0].shape
    group = 2 if experts % 2 == 0 else 1
    start = first // group
    tokens, width = slot.shape[2], w_down.shape[2]
    row = pl.BlockSpec((group, 1, tokens), lambda e, *_: (start + e, 0, 0))
    extra = [] if so_far is None else [so_far]
    return pl.pallas_call(
        functools.partial(combine_kernel, n_count=n_count, started=bool(extra)),
        grid_spec=pltpu.PrefetchScalarGridSpec(
            num_scalar_prefetch=1,
            grid=(experts // group,),
            in_specs=[row, row]
            + [pl.BlockSpec((group, slots, hid), lambda e, *_: (e, 0, 0)) for _ in hidden]
            + [
                pl.BlockSpec((group, hid, width), lambda e, place, j=j: (start + e, place[0] ^ j, 0))
                for j in range(n_count)
            ]
            + [whole(x.shape) for x in extra],
            out_specs=whole((tokens, width)),
            scratch_shapes=[pltpu.VMEM((tokens, width), F32), pltpu.VMEM((group * slots, width), BF16)],
        ),
        out_shape=jax.ShapeDtypeStruct((tokens, width), out_type),
        name="combine",
    )(place, slot, gate, *hidden, *[w_down] * n_count, *extra)


def routing(idx, packed, experts):
    stacked = jnp.concatenate(packed, axis=0)
    stacked = jnp.zeros_like(stacked).at[idx].set(stacked) if len(packed) == 1 else roll_wide(stacked)
    ids = stacked[:, :TOP].transpose(1, 0, 2).reshape(TOP, -1)
    gates = stacked[:, TOP:].transpose(1, 0, 2).reshape(TOP, -1)
    first = (lax.axis_index("wide") * experts).astype(F32)
    names = first + jnp.arange(experts, dtype=F32)
    same = ids[None] == names[:, None, None]
    member = jnp.any(same, axis=1)
    gate = jnp.sum(jnp.where(same, gates[None], 0.0), axis=1)
    tokens = ids.shape[1]
    before = (jnp.arange(tokens)[:, None] < jnp.arange(tokens)[None, :]).astype(BF16)
    rank = dot(member.astype(BF16), before).astype(jnp.int32)
    return jnp.where(member, rank, -1), gate


def roll_wide(stacked):
    count = stacked.shape[0]
    me = lax.axis_index("wide")
    return lax.dynamic_slice_in_dim(jnp.concatenate([stacked, stacked], axis=0), (count - me) % count, count, 0)


def body(
    residual,
    query_rows,
    key_rows,
    value_rows,
    segment_ids,
    o_weight,
    norm_gain,
    w_gate,
    w_up,
    w_down,
    expert_ids,
    gate_weights,
    target,
):
    w_count = lax.axis_size("wide")
    n_count = lax.axis_size("narrow")
    w_here = lax.axis_index("wide")
    n_here = lax.axis_index("narrow")
    tok_count, model_width = residual.shape
    part = tok_count // n_count
    experts = w_gate.shape[0]
    capacity = max(2, 2 * part * TOP // EXPERTS)
    slots = w_count * n_count * capacity
    out_width = o_weight.shape[1]

    attended = attend(query_rows, key_rows, value_rows, segment_ids)
    att_pieces, w_index = wide_pieces(attended)
    n_place = jnp.concatenate([n_here[None].astype(jnp.int32), w_index])
    w_place = jnp.concatenate([w_here[None].astype(jnp.int32), w_index])

    packed = jnp.concatenate([expert_ids.astype(F32).T, gate_weights.T], axis=0)
    packed, _ = lax.optimization_barrier((packed, attended))
    packed_pieces, _ = wide_pieces(packed)
    slot, gate = routing(w_index, packed_pieces, experts)
    by_place = slot.reshape(experts, w_count, n_count, part)
    slot_near = jnp.stack(
        [lax.dynamic_index_in_dim(by_place, n_here ^ j, 2, keepdims=False) for j in range(n_count)], axis=1
    ).reshape(experts, 1, -1)
    gain_here = lax.dynamic_slice_in_dim(norm_gain, w_here * out_width, out_width, 0)[None]

    shares = project(n_place, att_pieces, o_weight, n_count)
    own_resid = lax.dynamic_slice_in_dim(residual, n_here * part, part, 0)
    resid_pieces = wide_exchange(lambda w: lax.dynamic_slice_in_dim(own_resid, w * out_width, out_width, 1), shares[0])
    shares = [shares[0]] + [narrow_flip(shares[j], j) for j in range(1, n_count)]
    scaled = stream_of(n_place, gain_here, shares, resid_pieces).reshape(w_count * part, out_width)

    wide_rows, _ = wide_pieces(scaled)
    pieces = [narrow_pieces(rows)[0] for rows in wide_rows]
    if len(pieces) == 1 and w_count > 1:
        rows = jnp.stack(pieces[0]).transpose(0, 2, 1, 3).reshape(1, -1, model_width)
        pieces = [[rows]]
        w_place = jnp.stack([w_here, jnp.zeros_like(w_here)]).astype(jnp.int32)
    some = experts // PARTS if experts % (2 * PARTS) == 0 else experts
    norm, rows_of = norm_gain[None], []
    for first in range(0, experts, some):
        mine, norm = hidden_of(w_place, slot_near, norm, pieces, w_gate, w_up, slots, first, some)
        rows_of.append(mine)
    own_pieces, _ = lax.optimization_barrier(([group[0] for group in pieces], rows_of[-1]))
    base = base_of(w_place, norm_gain[None], target, own_pieces)
    partial_sum = None
    for i in range(len(rows_of)):
        later = i + 1 < len(rows_of)
        found, after = narrow_pieces(rows_of[i], (partial_sum, rows_of[i + 1] if later else None))
        partial_sum = after[0]
        if later:
            rows_of[i + 1] = after[1]
        out_type = F32 if later else BF16
        partial_sum = combine(n_place, slot[:, None], gate[:, None], found, w_down, i * some, partial_sum, out_type)
    returned = lax.all_to_all(
        partial_sum.reshape(w_count * n_count, part, -1),
        ("wide", "narrow"),
        split_axis=0,
        concat_axis=0,
        tiled=True,
    ).reshape(w_count, n_count, part, -1)
    moe_sum = jnp.sum(returned.astype(F32), axis=0).transpose(1, 0, 2)
    miss = base.reshape(moe_sum.shape) + moe_sum
    return jnp.sum(miss * miss, axis=(1, 2)) / model_width


def solution(mesh):
    return jax.shard_map(
        body,
        mesh=mesh,
        in_specs=(
            P(("groups", "wide"), None),
            P(("groups", "wide"), "narrow"),
            P(("groups", "wide"), "narrow"),
            P(("groups", "wide"), "narrow"),
            P(("groups", "wide"), None),
            P("narrow", "wide"),
            P(),
            P("wide", None, "narrow"),
            P("wide", None, "narrow"),
            P("wide", None, "narrow"),
            P(("groups", "wide"), None),
            P(("groups", "wide"), None),
            P(("groups", "wide", "narrow"), None),
        ),
        out_specs=P(("groups", "wide", "narrow")),
        check_vma=False,
    )
```

```python
import functools
import math

import jax
import jax.numpy as jnp
from jax import lax
from jax.experimental import pallas as pl
from jax.experimental.pallas import tpu as pltpu
from jax.sharding import PartitionSpec as P


HD = 128
EXPERTS = 32
TOP = 8
BF16 = jnp.bfloat16
F32 = jnp.float32
PARTS = 2
SPARE = 3 << 20
STREAMED = 50 << 20


def whole(shape):
    rank = len(shape)
    return pl.BlockSpec(shape, lambda *_: (0,) * rank, pipeline_mode=pl.Buffered(1))


def room(*arrays, twice=(), least=0):
    size = sum(a.size * a.dtype.itemsize for a in arrays) + 2 * sum(math.prod(n) * 2 for n in twice)
    return pltpu.CompilerParams(vmem_limit_bytes=min(60 << 20, max(least, size + SPARE)))


def dot(a, b, dims=((1,), (0,))):
    return lax.dot_general(a, b, (dims, ((), ())), preferred_element_type=F32)


def each(count, step):
    if count == 1:
        step(0)
    else:
        lax.fori_loop(0, count, lambda i, carry: (step(i), carry)[1], 0)


def chunk_of(total, most):
    return most if total % most == 0 else total


def wide_pieces(rows):
    count = lax.axis_size("wide")
    me = lax.axis_index("wide")
    if count > 8:
        return [lax.all_gather(rows, "wide", axis=0)], jnp.arange(count, dtype=jnp.int32)
    found = [rows[None]]
    for step in range(1, count):
        found.append(lax.ppermute(rows, "wide", [((i + step) % count, i) for i in range(count)])[None])
    return found, (me + jnp.arange(count, dtype=jnp.int32)) % count


def wide_exchange(block_of, after):
    count = lax.axis_size("wide")
    me = lax.axis_index("wide")
    if count > 8:
        stacked = jnp.stack([block_of(i) for i in range(count)])
        return [lax.all_to_all(stacked, "wide", split_axis=0, concat_axis=0, tiled=True)]
    found = [block_of(me)[None]]
    blocks, _ = lax.optimization_barrier(([block_of((me - step) % count) for step in range(1, count)], after))
    for step in range(1, count):
        pairs = [((i + step) % count, i) for i in range(count)]
        found.append(lax.ppermute(blocks[step - 1], "wide", pairs)[None])
    return found


def narrow_flip(rows, bit):
    count = lax.axis_size("narrow")
    return lax.ppermute(rows, "narrow", [(i, i ^ bit) for i in range(count)])


def narrow_pieces(rows, after=None):
    count = lax.axis_size("narrow")
    held = {0: rows}
    bit = count // 2
    while bit:
        for j in list(held):
            held[j ^ bit] = narrow_flip(held[j], bit)
        if after is not None and bit == count // 2:
            held[bit], after = lax.optimization_barrier((held[bit], after))
        bit //= 2
    return [held[j] for j in range(count)], after


def attend_kernel(q_ref, k_ref, v_ref, seg_ref, out_ref):
    tok_count, width = q_ref.shape
    seg = jnp.broadcast_to(seg_ref[...].astype(F32), (tok_count, tok_count))
    key_pos = lax.broadcasted_iota(jnp.int32, (tok_count, tok_count), 1)
    query_pos = lax.broadcasted_iota(jnp.int32, (tok_count, tok_count), 0)
    allowed = (seg == seg.T) & (key_pos <= query_pos)
    for h in range(width // HD):
        cols = slice(h * HD, (h + 1) * HD)
        scores = dot(q_ref[:, cols], k_ref[:, cols], ((1,), (1,))) * HD ** (-0.5)
        scores = jnp.where(allowed, scores, -jnp.inf)
        weights = jnp.exp(scores - jnp.max(scores, axis=1, keepdims=True))
        denom = jnp.sum(weights, axis=1, keepdims=True)
        out_ref[:, cols] = (dot(weights.astype(BF16), v_ref[:, cols]) / denom).astype(BF16)


def attend(q, k, v, seg):
    out_shape = jax.ShapeDtypeStruct(q.shape, BF16)
    grant = room(q, k, v, out_shape)
    return pl.pallas_call(attend_kernel, out_shape=out_shape, compiler_params=grant, name="attend")(q, k, v, seg)


def project_kernel(place_ref, *refs, pieces, n_count):
    att, w_ref, outs, product_ref = refs[:pieces], refs[pieces], refs[pieces + 1 : -1], refs[-1]
    me = place_ref[0]
    rows = jnp.concatenate([a[i] for a in att for i in range(a.shape[0])], axis=0)
    product_ref[...] = dot(rows, w_ref[...]).reshape(product_ref.shape)

    def spread(i, carry):
        w = place_ref[1 + i]
        for j in range(n_count):
            outs[j][w] = product_ref[i, me ^ j].astype(outs[j].dtype)
        return carry

    lax.fori_loop(0, product_ref.shape[0], spread, 0)


def project(place, att, o_weight, n_count):
    w_count = sum(a.shape[0] for a in att)
    tok_count, width = att[0].shape[1], o_weight.shape[1]
    shape = (w_count, tok_count // n_count, width)
    outs = [jax.ShapeDtypeStruct(shape, F32 if j == 0 else BF16) for j in range(n_count)]
    return pl.pallas_call(
        functools.partial(project_kernel, pieces=len(att), n_count=n_count),
        grid_spec=pltpu.PrefetchScalarGridSpec(
            num_scalar_prefetch=1,
            grid=(1,),
            in_specs=[whole(a.shape) for a in att] + [whole(o_weight.shape)],
            out_specs=[whole(shape) for _ in outs],
            scratch_shapes=[pltpu.VMEM((w_count, n_count, *shape[1:]), F32)],
        ),
        out_shape=outs,
        compiler_params=room(*att, o_weight, *outs, *outs, *outs),
        name="project",
    )(place, *att, o_weight)


def stream_kernel(place_ref, gain_ref, *refs, parts, pieces):
    shares, resid, out_ref = refs[:parts], refs[parts : parts + pieces], refs[parts + pieces]
    index = 0
    for a in resid:
        for i in range(a.shape[0]):
            w = place_ref[1 + index]
            index += 1
            total = a[i].astype(F32)
            for s in shares:
                total = total + s[w].astype(F32)
            out_ref[w] = (total * gain_ref[...]).astype(BF16)


def stream_of(place, gain_here, shares, resid):
    shape = shares[0].shape
    return pl.pallas_call(
        functools.partial(stream_kernel, parts=len(shares), pieces=len(resid)),
        grid_spec=pltpu.PrefetchScalarGridSpec(
            num_scalar_prefetch=1,
            grid=(1,),
            in_specs=[whole(gain_here.shape)] + [whole(a.shape) for a in (*shares, *resid)],
            out_specs=whole(shape),
        ),
        out_shape=jax.ShapeDtypeStruct(shape, BF16),
        compiler_params=room(*shares, *resid, shares[0]),
        name="stream",
    )(place, gain_here, *shares, *resid)


def base_kernel(place_ref, gain_ref, target_ref, *refs):
    pieces, base_ref = refs[:-1], refs[-1]
    width = pieces[0].shape[2]
    part = target_ref.shape[0]
    for i, piece in enumerate(pieces):
        col = pl.multiple_of(place_ref[1 + i] * width, 128)
        own = piece[0, pl.ds(pl.multiple_of(place_ref[0] * part, 8), part), :].astype(F32)
        base_ref[:, pl.ds(col, width)] = own / gain_ref[:, pl.ds(col, width)] - target_ref[:, pl.ds(col, width)].astype(F32)


def base_of(place, gain, target, pieces):
    return pl.pallas_call(
        base_kernel,
        grid_spec=pltpu.PrefetchScalarGridSpec(
            num_scalar_prefetch=1,
            grid=(1,),
            in_specs=[whole(a.shape) for a in (gain, target, *pieces)],
            out_specs=whole(target.shape),
        ),
        out_shape=jax.ShapeDtypeStruct(target.shape, F32),
        compiler_params=room(*pieces, target, target, target),
        name="base",
    )(place, gain, target, *pieces)


def hidden_kernel(place_ref, slot_ref, norm_ref, *refs, groups, first_call):
    total = sum(groups)
    pieces, wg_ref, wu_ref, out_ref = refs[:total], refs[total], refs[total + 1], refs[total + 2]
    rest = list(refs[total + 3 :])
    scale_ref = rest.pop(0) if first_call else norm_ref
    hidden_ref = rest.pop(0)
    tokens = scale_ref.shape[0]
    rows_ref = rest.pop(0) if total > 1 else pieces[0].at[0]
    model_width = wg_ref.shape[1]

    @pl.when(pl.program_id(0) == 0)
    def _():
        if total > 1:
            block, width = pieces[0].shape[1:]
            n_count, w_count = groups[0], len(groups)
            part = block // w_count
            for i in range(w_count):
                col = pl.multiple_of(place_ref[1 + i] * width, 128)
                for k in range(w_count):
                    source = pl.ds(pl.multiple_of(place_ref[1 + k] * part, part), part)
                    for j in range(n_count):
                        row = pl.multiple_of((k * n_count + (place_ref[0] ^ j)) * part, part)
                        rows_ref[pl.ds(row, part), pl.ds(col, width)] = pieces[i * n_count + j][0, source, :]
        if first_call:
            some = chunk_of(tokens, 64)
            wide = chunk_of(model_width, 1024)

            def scale_rows(c):
                here = pl.ds(pl.multiple_of(c * some, 16), some)
                sums = 0.0
                for first in range(0, model_width, wide):
                    inverse = 1.0 / norm_ref[:, first : first + wide]
                    stream = rows_ref[here, first : first + wide].astype(F32) * inverse
                    sums += jnp.sum(stream * stream, axis=1, keepdims=True)
                scale_ref[here, :] = jnp.broadcast_to(lax.rsqrt(sums / model_width + 1e-06), (some, 128))

            each(tokens // some, scale_rows)

    many = chunk_of(tokens, 256)

    def rows_done(c):
        here = pl.ds(pl.multiple_of(c * many, 128), many)
        rows = rows_ref[here, :]
        scale = scale_ref[here, :1]
        gate_val = dot(rows, wg_ref[0]) * scale
        up_val = dot(rows, wu_ref[0]) * scale
        hidden_ref[here, :] = (gate_val / (1.0 + jnp.exp(-gate_val)) * up_val).astype(BF16)

    each(tokens // many, rows_done)
    slots = out_ref.shape[1]
    few = chunk_of(slots, 128)

    def slots_done(c):
        first = pl.multiple_of(c * few, 16)
        slot = jnp.broadcast_to(slot_ref[0], (few, tokens))
        chosen = (lax.broadcasted_iota(jnp.int32, slot.shape, 0) + first == slot).astype(F32).astype(BF16)
        out_ref[0, pl.ds(first, few), :] = dot(chosen, hidden_ref[...]).astype(BF16)

    each(slots // few, slots_done)


def hidden_of(place, slot, norm, pieces, w_gate, w_up, slots, first, experts):
    model_width, hid = w_gate.shape[1:]
    flat = [p for group in pieces for p in group]
    tokens = slot.shape[2]
    weight = pl.BlockSpec((1, model_width, hid), lambda e, *_: (first + e, 0, 0))
    rows = [pltpu.VMEM((tokens, model_width), BF16)] if len(flat) > 1 else []
    out_specs = [pl.BlockSpec((1, slots, hid), lambda e, *_: (e, 0, 0))]
    out_shape = [jax.ShapeDtypeStruct((experts, slots, hid), BF16)]
    if first == 0:
        out_specs.append(whole((tokens, 128)))
        out_shape.append(jax.ShapeDtypeStruct((tokens, 128), F32))
    found = pl.pallas_call(
        functools.partial(hidden_kernel, groups=[len(g) for g in pieces], first_call=first == 0),
        grid_spec=pltpu.PrefetchScalarGridSpec(
            num_scalar_prefetch=1,
            grid=(experts,),
            in_specs=[pl.BlockSpec((1, 1, tokens), lambda e, *_: (first + e, 0, 0)), whole(norm.shape)]
            + [whole(p.shape) for p in flat]
            + [weight, weight],
            out_specs=out_specs,
            scratch_shapes=[pltpu.VMEM((tokens, hid), BF16)] + rows,
        ),
        out_shape=out_shape,
        compiler_params=room(
            *flat, *flat, slot, slot, slot, twice=[(model_width, hid)] * 2 + [(slots, hid), (tokens, 4 * hid)], least=STREAMED
        ),
        name="hidden",
    )(place, slot, norm, *flat, w_gate, w_up)
    return found if first == 0 else (found[0], norm)


def combine_kernel(place_ref, slot_ref, gate_ref, *refs, n_count, w_count, started):
    hidden, weights, rest = refs[:n_count], refs[n_count : 2 * n_count], refs[2 * n_count :]
    out_ref, sum_ref, result_ref = rest[-3:]
    group, slots, _ = hidden[0].shape

    @pl.when(pl.program_id(0) == 0)
    def _():
        sum_ref[...] = rest[0][...] if started else jnp.zeros_like(sum_ref)

    few = chunk_of(slots, 128)
    for e in range(group):

        def slots_done(c, e=e):
            here = pl.ds(pl.multiple_of(c * few, 16), few)
            result = 0.0
            for j in range(n_count):
                result += dot(hidden[j][e, here, :], weights[j][e])
            result_ref[pl.ds(pl.multiple_of(e * slots + c * few, 16), few), :] = result.astype(BF16)

        each(slots // few, slots_done)
    tokens = sum_ref.shape[0]
    many = chunk_of(tokens, 256)

    def rows_done(c):
        here = pl.ds(pl.multiple_of(c * many, 128), many)
        weight = []
        for e in range(group):
            slot = jnp.broadcast_to(slot_ref[e, :, here], (slots, many))
            gate = jnp.broadcast_to(gate_ref[e, :, here], (slots, many))
            weight.append(jnp.where(lax.broadcasted_iota(jnp.int32, slot.shape, 0) == slot, gate, 0.0))
        weight = jnp.concatenate(weight, axis=0) if group > 1 else weight[0]
        high = weight.astype(BF16)
        low = (weight - high.astype(F32)).astype(BF16)
        result = result_ref[...]
        sum_ref[here, :] += dot(high, result, ((0,), (0,))) + dot(low, result, ((0,), (0,)))

    each(tokens // many, rows_done)

    @pl.when(pl.program_id(0) == pl.num_programs(0) - 1)
    def _():
        if out_ref.dtype == F32:
            out_ref[...] = sum_ref[...]
        else:
            block = tokens // w_count
            for k in range(w_count):
                row = pl.multiple_of(place_ref[1 + k] * block, 16)
                out_ref[pl.ds(row, block), :] = sum_ref[k * block : (k + 1) * block, :].astype(BF16)


def combine(place, slot, gate, hidden, w_down, first, so_far, out_type):
    n_count = len(hidden)
    experts, slots, hid = hidden[0].shape
    group = 2 if experts % 2 == 0 else 1
    start = first // group
    tokens, width = slot.shape[2], w_down.shape[2]
    row = pl.BlockSpec((group, 1, tokens), lambda e, *_: (start + e, 0, 0))
    extra = [] if so_far is None else [so_far]
    return pl.pallas_call(
        functools.partial(combine_kernel, n_count=n_count, w_count=place.shape[0] - 1, started=bool(extra)),
        grid_spec=pltpu.PrefetchScalarGridSpec(
            num_scalar_prefetch=1,
            grid=(experts // group,),
            in_specs=[row, row]
            + [pl.BlockSpec((group, slots, hid), lambda e, *_: (e, 0, 0)) for _ in hidden]
            + [
                pl.BlockSpec((group, hid, width), lambda e, place, j=j: (start + e, place[0] ^ j, 0))
                for j in range(n_count)
            ]
            + [whole(x.shape) for x in extra],
            out_specs=whole((tokens, width)),
            scratch_shapes=[pltpu.VMEM((tokens, width), F32), pltpu.VMEM((group * slots, width), BF16)],
        ),
        out_shape=jax.ShapeDtypeStruct((tokens, width), out_type),
        compiler_params=room(
            twice=[(group * hid * n_count, width), (group * n_count * slots, hid)] + [(tokens, width)] * 4
            + [(group * slots, width)] * 2 + [(group * slots, chunk_of(tokens, 256))] * 4,
            least=STREAMED,
        ),
        name="combine",
    )(place, slot, gate, *hidden, *[w_down] * n_count, *extra)


def route_kernel(place_ref, packed_ref, slot_ref, gate_ref):
    experts, _, tokens = slot_ref.shape
    ids, gates = packed_ref[:TOP, :], packed_ref[TOP:, :]
    member = []
    for e in range(experts):
        same = ids == (place_ref[0] * experts + e).astype(F32)
        member.append(jnp.max(same.astype(F32), axis=0, keepdims=True))
        gate_ref[e] = jnp.sum(jnp.where(same, gates, 0.0), axis=0, keepdims=True)
    member = jnp.concatenate(member, axis=0) if experts > 1 else member[0]
    some = chunk_of(tokens, 256)
    for first in range(0, tokens, some):
        row = lax.broadcasted_iota(jnp.int32, (tokens, some), 0)
        before = (row < lax.broadcasted_iota(jnp.int32, (tokens, some), 1) + first).astype(F32).astype(BF16)
        rank = dot(member.astype(BF16), before)
        found = jnp.where(member[:, first : first + some] > 0, rank, -1.0).astype(jnp.int32)
        for e in range(experts):
            slot_ref[e, :, first : first + some] = found[e : e + 1]


def routing(place, packed, experts):
    tokens = packed.shape[1]
    out_shape = [jax.ShapeDtypeStruct((experts, 1, tokens), t) for t in (jnp.int32, F32)]
    return pl.pallas_call(
        route_kernel,
        grid_spec=pltpu.PrefetchScalarGridSpec(
            num_scalar_prefetch=1,
            grid=(1,),
            in_specs=[whole(packed.shape)],
            out_specs=[whole(o.shape) for o in out_shape],
        ),
        out_shape=out_shape,
        compiler_params=room(packed, *out_shape, twice=[(tokens, chunk_of(tokens, 256))] * 4),
        name="route",
    )(place, packed)


def body(
    residual,
    query_rows,
    key_rows,
    value_rows,
    segment_ids,
    o_weight,
    norm_gain,
    w_gate,
    w_up,
    w_down,
    expert_ids,
    gate_weights,
    target,
):
    w_count = lax.axis_size("wide")
    n_count = lax.axis_size("narrow")
    w_here = lax.axis_index("wide")
    n_here = lax.axis_index("narrow")
    tok_count, model_width = residual.shape
    part = tok_count // n_count
    experts = w_gate.shape[0]
    capacity = max(2, 2 * part * TOP // EXPERTS)
    slots = w_count * n_count * capacity
    out_width = o_weight.shape[1]

    attended = attend(query_rows, key_rows, value_rows, segment_ids)
    att_pieces, w_index = wide_pieces(attended)
    n_place = jnp.concatenate([n_here[None].astype(jnp.int32), w_index])
    w_place = jnp.concatenate([w_here[None].astype(jnp.int32), w_index])

    packed = jnp.concatenate([expert_ids.astype(F32).T, gate_weights.T], axis=0)
    packed, _ = lax.optimization_barrier((packed, attended))
    packed_pieces, _ = wide_pieces(packed)
    shares = project(n_place, att_pieces, o_weight, n_count)
    packed_pieces, _ = lax.optimization_barrier((packed_pieces, shares[0]))
    each_wide = [piece[i] for piece in packed_pieces for i in range(piece.shape[0])]
    slot, gate = routing(w_place, jnp.concatenate(each_wide, axis=1), experts)
    gain_here = lax.dynamic_slice_in_dim(norm_gain, w_here * out_width, out_width, 0)[None]
    own_resid = lax.dynamic_slice_in_dim(residual, n_here * part, part, 0)
    resid_pieces = wide_exchange(lambda w: lax.dynamic_slice_in_dim(own_resid, w * out_width, out_width, 1), shares[0])
    shares = [shares[0]] + [narrow_flip(shares[j], j) for j in range(1, n_count)]
    shares, slot, gate = lax.optimization_barrier((shares, slot, gate))
    scaled = stream_of(n_place, gain_here, shares, resid_pieces).reshape(w_count * part, out_width)

    wide_rows, _ = wide_pieces(scaled)
    pieces = [narrow_pieces(rows)[0] for rows in wide_rows]
    if len(pieces) == 1 and w_count > 1:
        rows = jnp.stack(pieces[0])[n_here ^ jnp.arange(n_count)].reshape(n_count, w_count, w_count, part, -1)
        pieces = [[rows.transpose(2, 0, 3, 1, 4).reshape(1, -1, model_width)]]
        own_place = jnp.stack([w_here * n_count + n_here, jnp.zeros_like(w_here)]).astype(jnp.int32)
    else:
        own_place = w_place
    some = experts // PARTS if experts % (2 * PARTS) == 0 else experts
    norm, rows_of = norm_gain[None], []
    for first in range(0, experts, some):
        mine, norm = hidden_of(n_place, slot, norm, pieces, w_gate, w_up, slots, first, some)
        rows_of.append(mine)
    own_pieces, _ = lax.optimization_barrier(([group[0] for group in pieces], rows_of[-1]))
    base = base_of(own_place, norm_gain[None], target, own_pieces)
    partial_sum = None
    for i in range(len(rows_of)):
        later = i + 1 < len(rows_of)
        found, after = narrow_pieces(rows_of[i], (partial_sum, rows_of[i + 1] if later else None))
        partial_sum = after[0]
        if later:
            rows_of[i + 1] = after[1]
        out_type = F32 if later else BF16
        partial_sum = combine(n_place, slot, gate, found, w_down, i * some, partial_sum, out_type)
    returned = lax.all_to_all(
        partial_sum.reshape(w_count * n_count, part, -1),
        ("wide", "narrow"),
        split_axis=0,
        concat_axis=0,
        tiled=True,
    ).reshape(w_count, n_count, part, -1)
    moe_sum = jnp.sum(returned.astype(F32), axis=0).transpose(1, 0, 2)
    miss = base.reshape(moe_sum.shape) + moe_sum
    return jnp.sum(miss * miss, axis=(1, 2)) / model_width


def solution(mesh):
    return jax.shard_map(
        body,
        mesh=mesh,
        in_specs=(
            P(("groups", "wide"), None),
            P(("groups", "wide"), "narrow"),
            P(("groups", "wide"), "narrow"),
            P(("groups", "wide"), "narrow"),
            P(("groups", "wide"), None),
            P("narrow", "wide"),
            P(),
            P("wide", None, "narrow"),
            P("wide", None, "narrow"),
            P("wide", None, "narrow"),
            P(("groups", "wide"), None),
            P(("groups", "wide"), None),
            P(("groups", "wide", "narrow"), None),
        ),
        out_specs=P(("groups", "wide", "narrow")),
        check_vma=False,
    )
```

```python
import functools
import math

import jax
import jax.numpy as jnp
from jax import lax
from jax.experimental import pallas as pl
from jax.experimental.pallas import tpu as pltpu
from jax.sharding import PartitionSpec as P


HD = 128
EXPERTS = 32
TOP = 8
BF16 = jnp.bfloat16
F32 = jnp.float32
PARTS = 2
SPARE = 3 << 20
STREAMED = 50 << 20


def whole(shape):
    rank = len(shape)
    return pl.BlockSpec(shape, lambda *_: (0,) * rank, pipeline_mode=pl.Buffered(1))


def room(*arrays, twice=(), least=0):
    size = sum(a.size * a.dtype.itemsize for a in arrays) + 2 * sum(math.prod(n) * 2 for n in twice)
    return pltpu.CompilerParams(vmem_limit_bytes=min(60 << 20, max(least, size + SPARE)))


def dot(a, b, dims=((1,), (0,))):
    return lax.dot_general(a, b, (dims, ((), ())), preferred_element_type=F32)


def each(count, step):
    if count == 1:
        step(0)
    else:
        lax.fori_loop(0, count, lambda i, carry: (step(i), carry)[1], 0)


def chunk_of(total, most):
    return most if total % most == 0 else total


def wide_pieces(rows):
    count = lax.axis_size("wide")
    me = lax.axis_index("wide")
    if count > 8:
        return [lax.all_gather(rows, "wide", axis=0)], jnp.arange(count, dtype=jnp.int32)
    found = [rows[None]]
    for step in range(1, count):
        found.append(lax.ppermute(rows, "wide", [((i + step) % count, i) for i in range(count)])[None])
    return found, (me + jnp.arange(count, dtype=jnp.int32)) % count


def wide_exchange(block_of, after):
    count = lax.axis_size("wide")
    me = lax.axis_index("wide")
    if count > 8:
        stacked = jnp.stack([block_of(i) for i in range(count)])
        return [lax.all_to_all(stacked, "wide", split_axis=0, concat_axis=0, tiled=True)]
    found = [block_of(me)[None]]
    blocks, _ = lax.optimization_barrier(([block_of((me - step) % count) for step in range(1, count)], after))
    for step in range(1, count):
        pairs = [((i + step) % count, i) for i in range(count)]
        found.append(lax.ppermute(blocks[step - 1], "wide", pairs)[None])
    return found


def narrow_flip(rows, bit):
    count = lax.axis_size("narrow")
    return lax.ppermute(rows, "narrow", [(i, i ^ bit) for i in range(count)])


def narrow_pieces(rows, after=None):
    count = lax.axis_size("narrow")
    held = {0: rows}
    bit = count // 2
    while bit:
        for j in list(held):
            held[j ^ bit] = narrow_flip(held[j], bit)
        if after is not None and bit == count // 2:
            held[bit], after = lax.optimization_barrier((held[bit], after))
        bit //= 2
    return [held[j] for j in range(count)], after


def attend_kernel(q_ref, k_ref, v_ref, seg_ref, out_ref):
    tok_count, width = q_ref.shape
    seg = jnp.broadcast_to(seg_ref[...].astype(F32), (tok_count, tok_count))
    key_pos = lax.broadcasted_iota(jnp.int32, (tok_count, tok_count), 1)
    query_pos = lax.broadcasted_iota(jnp.int32, (tok_count, tok_count), 0)
    allowed = (seg == seg.T) & (key_pos <= query_pos)
    for h in range(width // HD):
        cols = slice(h * HD, (h + 1) * HD)
        scores = dot(q_ref[:, cols], k_ref[:, cols], ((1,), (1,))) * HD ** (-0.5)
        scores = jnp.where(allowed, scores, -jnp.inf)
        weights = jnp.exp(scores - jnp.max(scores, axis=1, keepdims=True))
        denom = jnp.sum(weights, axis=1, keepdims=True)
        out_ref[:, cols] = (dot(weights.astype(BF16), v_ref[:, cols]) / denom).astype(BF16)


def attend(q, k, v, seg):
    return pl.pallas_call(attend_kernel, out_shape=jax.ShapeDtypeStruct(q.shape, BF16), name="attend")(q, k, v, seg)


def project_kernel(place_ref, *refs, pieces, n_count):
    att, w_ref, outs, product_ref = refs[:pieces], refs[pieces], refs[pieces + 1 : -1], refs[-1]
    me = place_ref[0]
    rows = jnp.concatenate([a[i] for a in att for i in range(a.shape[0])], axis=0)
    product_ref[...] = dot(rows, w_ref[...]).reshape(product_ref.shape)

    def spread(i, carry):
        w = place_ref[1 + i]
        for j in range(n_count):
            outs[j][w] = product_ref[i, me ^ j].astype(outs[j].dtype)
        return carry

    lax.fori_loop(0, product_ref.shape[0], spread, 0)


def project(place, att, o_weight, n_count):
    w_count = sum(a.shape[0] for a in att)
    tok_count, width = att[0].shape[1], o_weight.shape[1]
    shape = (w_count, tok_count // n_count, width)
    outs = [jax.ShapeDtypeStruct(shape, F32 if j == 0 else BF16) for j in range(n_count)]
    return pl.pallas_call(
        functools.partial(project_kernel, pieces=len(att), n_count=n_count),
        grid_spec=pltpu.PrefetchScalarGridSpec(
            num_scalar_prefetch=1,
            grid=(1,),
            in_specs=[whole(a.shape) for a in att] + [whole(o_weight.shape)],
            out_specs=[whole(shape) for _ in outs],
            scratch_shapes=[pltpu.VMEM((w_count, n_count, *shape[1:]), F32)],
        ),
        out_shape=outs,
        compiler_params=room(*att, o_weight, *outs, *outs, *outs),
        name="project",
    )(place, *att, o_weight)


def stream_kernel(place_ref, gain_ref, *refs, parts, pieces):
    shares, resid, out_ref = refs[:parts], refs[parts : parts + pieces], refs[parts + pieces]
    index = 0
    for a in resid:
        for i in range(a.shape[0]):
            w = place_ref[1 + index]
            index += 1
            total = a[i].astype(F32)
            for s in shares:
                total = total + s[w].astype(F32)
            out_ref[w] = (total * gain_ref[...]).astype(BF16)


def stream_of(place, gain_here, shares, resid):
    shape = shares[0].shape
    return pl.pallas_call(
        functools.partial(stream_kernel, parts=len(shares), pieces=len(resid)),
        grid_spec=pltpu.PrefetchScalarGridSpec(
            num_scalar_prefetch=1,
            grid=(1,),
            in_specs=[whole(gain_here.shape)] + [whole(a.shape) for a in (*shares, *resid)],
            out_specs=whole(shape),
        ),
        out_shape=jax.ShapeDtypeStruct(shape, BF16),
        compiler_params=room(*shares, *resid, shares[0]),
        name="stream",
    )(place, gain_here, *shares, *resid)


def base_kernel(place_ref, inverse_ref, target_ref, *refs):
    pieces, base_ref = refs[:-1], refs[-1]
    width = pieces[0].shape[2]
    part = target_ref.shape[0]
    for i, piece in enumerate(pieces):
        col = pl.multiple_of(place_ref[1 + i] * width, 128)
        own = piece[0, pl.ds(pl.multiple_of(place_ref[0] * part, 8), part), :].astype(F32)
        base_ref[:, pl.ds(col, width)] = own * inverse_ref[:, pl.ds(col, width)] - target_ref[:, pl.ds(col, width)].astype(F32)


def base_of(place, gain, target, pieces):
    return pl.pallas_call(
        base_kernel,
        grid_spec=pltpu.PrefetchScalarGridSpec(
            num_scalar_prefetch=1,
            grid=(1,),
            in_specs=[whole(a.shape) for a in (gain, target, *pieces)],
            out_specs=whole(target.shape),
        ),
        out_shape=jax.ShapeDtypeStruct(target.shape, F32),
        compiler_params=room(*pieces, target, target, target),
        name="base",
    )(place, gain, target, *pieces)


def hidden_kernel(place_ref, slot_ref, norm_ref, *refs, groups, first_call):
    total = sum(groups)
    pieces, wg_ref, wu_ref, out_ref = refs[:total], refs[total], refs[total + 1], refs[total + 2]
    rest = list(refs[total + 3 :])
    scale_ref = rest.pop(0) if first_call else norm_ref
    hidden_ref = rest.pop(0)
    tokens = scale_ref.shape[0]
    rows_ref = rest.pop(0) if total > 1 else pieces[0].at[0]
    model_width = wg_ref.shape[1]

    @pl.when(pl.program_id(0) == 0)
    def _():
        if total > 1:
            block, width = pieces[0].shape[1:]
            n_count, w_count = groups[0], len(groups)
            part = block // w_count
            for i in range(w_count):
                col = pl.multiple_of(place_ref[1 + i] * width, 128)
                for k in range(w_count):
                    source = pl.ds(pl.multiple_of(place_ref[1 + k] * part, part), part)
                    for j in range(n_count):
                        row = pl.multiple_of((k * n_count + (place_ref[0] ^ j)) * part, part)
                        rows_ref[pl.ds(row, part), pl.ds(col, width)] = pieces[i * n_count + j][0, source, :]
        if first_call:
            some = chunk_of(tokens, 64)
            wide = chunk_of(model_width, 1024)

            def scale_rows(c):
                here = pl.ds(pl.multiple_of(c * some, 16), some)
                sums = 0.0
                for first in range(0, model_width, wide):
                    stream = rows_ref[here, first : first + wide].astype(F32) * norm_ref[:, first : first + wide]
                    sums += jnp.sum(stream * stream, axis=1, keepdims=True)
                scale_ref[here, :] = jnp.broadcast_to(lax.rsqrt(sums / model_width + 1e-06), (some, 128))

            each(tokens // some, scale_rows)

    many = chunk_of(tokens, 256)

    def rows_done(c):
        here = pl.ds(pl.multiple_of(c * many, 128), many)
        rows = rows_ref[here, :]
        scale = scale_ref[here, :1]
        gate_val = dot(rows, wg_ref[0]) * scale
        up_val = dot(rows, wu_ref[0]) * scale
        hidden_ref[here, :] = (gate_val / (1.0 + jnp.exp(-gate_val)) * up_val).astype(BF16)

    each(tokens // many, rows_done)
    slots = out_ref.shape[1]
    few = chunk_of(slots, 128)

    def slots_done(c):
        first = pl.multiple_of(c * few, 16)
        slot = jnp.broadcast_to(slot_ref[0], (few, tokens))
        chosen = (lax.broadcasted_iota(jnp.int32, slot.shape, 0) + first == slot).astype(F32).astype(BF16)
        out_ref[0, pl.ds(first, few), :] = dot(chosen, hidden_ref[...]).astype(BF16)

    each(slots // few, slots_done)


def hidden_of(place, slot, norm, pieces, w_gate, w_up, slots, first, experts):
    model_width, hid = w_gate.shape[1:]
    flat = [p for group in pieces for p in group]
    tokens = slot.shape[2]
    weight = pl.BlockSpec((1, model_width, hid), lambda e, *_: (first + e, 0, 0))
    rows = [pltpu.VMEM((tokens, model_width), BF16)] if len(flat) > 1 else []
    out_specs = [pl.BlockSpec((1, slots, hid), lambda e, *_: (e, 0, 0))]
    out_shape = [jax.ShapeDtypeStruct((experts, slots, hid), BF16)]
    if first == 0:
        out_specs.append(whole((tokens, 128)))
        out_shape.append(jax.ShapeDtypeStruct((tokens, 128), F32))
    found = pl.pallas_call(
        functools.partial(hidden_kernel, groups=[len(g) for g in pieces], first_call=first == 0),
        grid_spec=pltpu.PrefetchScalarGridSpec(
            num_scalar_prefetch=1,
            grid=(experts,),
            in_specs=[pl.BlockSpec((1, 1, tokens), lambda e, *_: (first + e, 0, 0)), whole(norm.shape)]
            + [whole(p.shape) for p in flat]
            + [weight, weight],
            out_specs=out_specs,
            scratch_shapes=[pltpu.VMEM((tokens, hid), BF16)] + rows,
        ),
        out_shape=out_shape,
        compiler_params=room(
            *flat, *flat, slot, slot, slot, twice=[(model_width, hid)] * 2 + [(slots, hid), (tokens, 4 * hid)], least=STREAMED
        ),
        name="hidden",
    )(place, slot, norm, *flat, w_gate, w_up)
    return found if first == 0 else (found[0], norm)


def combine_kernel(place_ref, slot_ref, gate_ref, *refs, n_count, w_count, started):
    hidden, weights, rest = refs[:n_count], refs[n_count : 2 * n_count], refs[2 * n_count :]
    out_ref, sum_ref, result_ref = rest[-3:]
    group, slots, _ = hidden[0].shape

    @pl.when(pl.program_id(0) == 0)
    def _():
        sum_ref[...] = rest[0][...] if started else jnp.zeros_like(sum_ref)

    few = chunk_of(slots, 128)
    for e in range(group):

        def slots_done(c, e=e):
            here = pl.ds(pl.multiple_of(c * few, 16), few)
            result = 0.0
            for j in range(n_count):
                result += dot(hidden[j][e, here, :], weights[j][e])
            result_ref[pl.ds(pl.multiple_of(e * slots + c * few, 16), few), :] = result.astype(BF16)

        each(slots // few, slots_done)
    tokens = sum_ref.shape[0]
    many = chunk_of(tokens, 256)

    def rows_done(c):
        here = pl.ds(pl.multiple_of(c * many, 128), many)
        weight = []
        for e in range(group):
            slot = jnp.broadcast_to(slot_ref[e, :, here], (slots, many))
            gate = jnp.broadcast_to(gate_ref[e, :, here], (slots, many))
            weight.append(jnp.where(lax.broadcasted_iota(jnp.int32, slot.shape, 0) == slot, gate, 0.0))
        weight = jnp.concatenate(weight, axis=0) if group > 1 else weight[0]
        high = weight.astype(BF16)
        low = (weight - high.astype(F32)).astype(BF16)
        result = result_ref[...]
        sum_ref[here, :] += dot(high, result, ((0,), (0,))) + dot(low, result, ((0,), (0,)))

    each(tokens // many, rows_done)

    @pl.when(pl.program_id(0) == pl.num_programs(0) - 1)
    def _():
        if out_ref.dtype == F32:
            out_ref[...] = sum_ref[...]
        else:
            block = tokens // w_count
            for k in range(w_count):
                row = pl.multiple_of(place_ref[1 + k] * block, 16)
                out_ref[pl.ds(row, block), :] = sum_ref[k * block : (k + 1) * block, :].astype(BF16)


def combine(place, slot, gate, hidden, w_down, first, so_far, out_type):
    n_count = len(hidden)
    experts, slots, hid = hidden[0].shape
    group = 2 if experts % 2 == 0 else 1
    start = first // group
    tokens, width = slot.shape[2], w_down.shape[2]
    row = pl.BlockSpec((group, 1, tokens), lambda e, *_: (start + e, 0, 0))
    extra = [] if so_far is None else [so_far]
    return pl.pallas_call(
        functools.partial(combine_kernel, n_count=n_count, w_count=place.shape[0] - 1, started=bool(extra)),
        grid_spec=pltpu.PrefetchScalarGridSpec(
            num_scalar_prefetch=1,
            grid=(experts // group,),
            in_specs=[row, row]
            + [pl.BlockSpec((group, slots, hid), lambda e, *_: (e, 0, 0)) for _ in hidden]
            + [
                pl.BlockSpec((group, hid, width), lambda e, place, j=j: (start + e, place[0] ^ j, 0))
                for j in range(n_count)
            ]
            + [whole(x.shape) for x in extra],
            out_specs=whole((tokens, width)),
            scratch_shapes=[pltpu.VMEM((tokens, width), F32), pltpu.VMEM((group * slots, width), BF16)],
        ),
        out_shape=jax.ShapeDtypeStruct((tokens, width), out_type),
        compiler_params=room(
            twice=[(group * hid * n_count, width), (group * n_count * slots, hid)] + [(tokens, width)] * 4
            + [(group * slots, width)] * 2 + [(group * slots, chunk_of(tokens, 256))] * 4,
            least=STREAMED,
        ),
        name="combine",
    )(place, slot, gate, *hidden, *[w_down] * n_count, *extra)


def route_kernel(place_ref, packed_ref, slot_ref, gate_ref):
    experts, _, tokens = slot_ref.shape
    ids, gates = packed_ref[:TOP, :], packed_ref[TOP:, :]
    member = []
    for e in range(experts):
        same = ids == (place_ref[0] * experts + e).astype(F32)
        member.append(jnp.max(same.astype(F32), axis=0, keepdims=True))
        gate_ref[e] = jnp.sum(jnp.where(same, gates, 0.0), axis=0, keepdims=True)
    member = jnp.concatenate(member, axis=0) if experts > 1 else member[0]
    some = chunk_of(tokens, 256)
    for first in range(0, tokens, some):
        row = lax.broadcasted_iota(jnp.int32, (tokens, some), 0)
        before = (row < lax.broadcasted_iota(jnp.int32, (tokens, some), 1) + first).astype(F32).astype(BF16)
        rank = dot(member.astype(BF16), before)
        found = jnp.where(member[:, first : first + some] > 0, rank, -1.0).astype(jnp.int32)
        for e in range(experts):
            slot_ref[e, :, first : first + some] = found[e : e + 1]


def routing(place, packed, experts):
    tokens = packed.shape[1]
    out_shape = [jax.ShapeDtypeStruct((experts, 1, tokens), t) for t in (jnp.int32, F32)]
    return pl.pallas_call(
        route_kernel,
        grid_spec=pltpu.PrefetchScalarGridSpec(
            num_scalar_prefetch=1,
            grid=(1,),
            in_specs=[whole(packed.shape)],
            out_specs=[whole(o.shape) for o in out_shape],
        ),
        out_shape=out_shape,
        compiler_params=room(packed, *out_shape, twice=[(tokens, chunk_of(tokens, 256))] * 4),
        name="route",
    )(place, packed)


def body(
    residual,
    query_rows,
    key_rows,
    value_rows,
    segment_ids,
    o_weight,
    norm_gain,
    w_gate,
    w_up,
    w_down,
    expert_ids,
    gate_weights,
    target,
):
    w_count = lax.axis_size("wide")
    n_count = lax.axis_size("narrow")
    w_here = lax.axis_index("wide")
    n_here = lax.axis_index("narrow")
    tok_count, model_width = residual.shape
    part = tok_count // n_count
    experts = w_gate.shape[0]
    capacity = max(2, 2 * part * TOP // EXPERTS)
    slots = w_count * n_count * capacity
    out_width = o_weight.shape[1]

    attended = attend(query_rows, key_rows, value_rows, segment_ids)
    att_pieces, w_index = wide_pieces(attended)
    n_place = jnp.concatenate([n_here[None].astype(jnp.int32), w_index])
    w_place = jnp.concatenate([w_here[None].astype(jnp.int32), w_index])

    own_resid = lax.dynamic_slice_in_dim(residual, n_here * part, part, 0)
    resid_pieces = wide_exchange(lambda w: lax.dynamic_slice_in_dim(own_resid, w * out_width, out_width, 1), attended)
    gain_here = lax.dynamic_slice_in_dim(norm_gain, w_here * out_width, out_width, 0)[None]
    inverse = 1.0 / norm_gain[None]
    packed = jnp.concatenate([expert_ids.astype(F32).T, gate_weights.T], axis=0)
    packed, gain_here, inverse, att_pieces = lax.optimization_barrier((packed, gain_here, inverse, att_pieces))

    shares = project(n_place, att_pieces, o_weight, n_count)
    shares = [shares[0]] + [narrow_flip(shares[j], j) for j in range(1, n_count)]
    scaled = stream_of(n_place, gain_here, shares, resid_pieces).reshape(w_count * part, out_width)

    wide_rows, _ = wide_pieces(scaled)
    pieces = []
    for rows in wide_rows:
        pieces.append(narrow_pieces(rows)[0])
    packed, _ = lax.optimization_barrier((packed, scaled))
    packed_pieces, _ = wide_pieces(packed)
    each_wide = [piece[i] for piece in packed_pieces for i in range(piece.shape[0])]
    slot, gate = routing(w_place, jnp.concatenate(each_wide, axis=1), experts)
    if len(pieces) == 1 and w_count > 1:
        rows = jnp.stack(pieces[0])[n_here ^ jnp.arange(n_count)].reshape(n_count, w_count, w_count, part, -1)
        pieces = [[rows.transpose(2, 0, 3, 1, 4).reshape(1, -1, model_width)]]
        own_place = jnp.stack([w_here * n_count + n_here, jnp.zeros_like(w_here)]).astype(jnp.int32)
    else:
        own_place = w_place
    some = experts // PARTS if experts % (2 * PARTS) == 0 else experts
    norm, rows_of = inverse, []
    for first in range(0, experts, some):
        mine, norm = hidden_of(n_place, slot, norm, pieces, w_gate, w_up, slots, first, some)
        rows_of.append(mine)
    own_pieces, _ = lax.optimization_barrier(([group[0] for group in pieces], rows_of[-1]))
    base = base_of(own_place, inverse, target, own_pieces)
    partial_sum = None
    for i in range(len(rows_of)):
        later = i + 1 < len(rows_of)
        found, after = narrow_pieces(rows_of[i], (partial_sum, rows_of[i + 1] if later else None))
        partial_sum = after[0]
        if later:
            rows_of[i + 1] = after[1]
        out_type = F32 if later else BF16
        partial_sum = combine(n_place, slot, gate, found, w_down, i * some, partial_sum, out_type)
    returned = lax.all_to_all(
        partial_sum.reshape(w_count * n_count, part, -1),
        ("wide", "narrow"),
        split_axis=0,
        concat_axis=0,
        tiled=True,
    ).reshape(w_count, n_count, part, -1)
    moe_sum = jnp.sum(returned.astype(F32), axis=0).transpose(1, 0, 2)
    miss = base.reshape(moe_sum.shape) + moe_sum
    return jnp.sum(miss * miss, axis=(1, 2)) / model_width


def solution(mesh):
    return jax.shard_map(
        body,
        mesh=mesh,
        in_specs=(
            P(("groups", "wide"), None),
            P(("groups", "wide"), "narrow"),
            P(("groups", "wide"), "narrow"),
            P(("groups", "wide"), "narrow"),
            P(("groups", "wide"), None),
            P("narrow", "wide"),
            P(),
            P("wide", None, "narrow"),
            P("wide", None, "narrow"),
            P("wide", None, "narrow"),
            P(("groups", "wide"), None),
            P(("groups", "wide"), None),
            P(("groups", "wide", "narrow"), None),
        ),
        out_specs=P(("groups", "wide", "narrow")),
        check_vma=False,
    )
```
